32 devices in a mesh: groups: 2 (over y), frame: 4 (over z), strip: 2 (over x), slab: 2 (over core).
Axes of the slice: x: 2, y: 2, z: 4, core: 2. Of those that a mesh axis runs over, the one named last changes fastest.
Arguments:
- frames_in: bfloat16 [16, 8, 128, 192], P(('groups', 'frame'), 'strip', 'slab'), parts along dimension 0, may hold values from -6 to 6
- weight_first: bfloat16 [3, 3, 3, 192, 192], replicated, may hold values from -0.078125 to 0.078125
- scale_first: float32 [192], replicated, may hold values from 0.25 to 1.75
- weight_second: bfloat16 [3, 3, 3, 192, 192], replicated, may hold values from -0.078125 to 0.078125
- scale_second: float32 [192], replicated, may hold values from 0.25 to 1.75
Outputs:
- latents_out: bfloat16 [16, 8, 128, 192], P(('groups', 'frame'), 'strip', 'slab'), parts along dimension 0
The draws below stay inside these ranges and needn't reach their ends.
There are 2 independent parts, one for each index of `groups`. The reference program is written for one: setup_inputs(seed, part) draws one part's arguments, and reference() takes and returns one part's arrays. A program takes and returns all parts, laid end to end along the dimension named above; an argument that names none is the same for every part. Nothing has to cross between parts.
All inputs are finite; a program needn't handle non-finite values.
Results may differ from the reference program's by a relative error of at most 0.0051.
Values may be sent and summed in bfloat16 or wider, within the bound.
A program may use at most 64 MiB of HBM per device.

```python
import jax
import jax.numpy as jnp
from jax import lax

C = 192
NF = 8
NH = 8
NW = 128


def block_scale(rng, shape, cuts, smallest, largest):
    level, own = 1.0, jax.random.fold_in(rng, 6)
    for position, shards_of in cuts:
        heights = jnp.exp(jax.random.uniform(jax.random.fold_in(own, position), (shards_of,), jnp.float32, smallest / len(cuts), largest / len(cuts)))
        level = level * jnp.repeat(heights, shape[position] // shards_of).reshape([-1 if axis == position else 1 for axis in range(len(shape))])
    return level


def noise(rng, dims, scale, most, cuts=(), held_as=jnp.bfloat16):
    drawn = jax.random.normal(rng, dims, jnp.float32) * scale
    if len(cuts) > 0:
        drawn = block_scale(rng, dims, cuts, -0.22, 0.18) * drawn
    return jnp.clip(drawn, min=-most, max=most).astype(held_as)


def setup_inputs(seed: int = 0, part: int = 0) -> dict:
    splits = jax.random.split(jax.random.key(seed), 6)
    part_keys = jax.random.split(jax.random.fold_in(splits[5], part), 6)
    frames_in = noise(part_keys[0], (NF, NH, NW, C), 1.0, 6.0, ((0, 4), (1, 2), (2, 2)))
    weight_first = noise(splits[1], (3, 3, 3, C, C), (27 * C) ** -0.5, 0.078125)
    scale_first = jnp.clip(1.0 + 0.15 * jax.random.normal(splits[2], (C,), jnp.float32), 0.25, 1.75)
    weight_second = noise(splits[3], (3, 3, 3, C, C), (27 * C) ** -0.5, 0.078125)
    scale_second = jnp.clip(1.0 + 0.15 * jax.random.normal(splits[4], (C,), jnp.float32), 0.25, 1.75)
    return {"frames_in": frames_in, "weight_first": weight_first, "scale_first": scale_first, "weight_second": weight_second, "scale_second": scale_second}


def tap_rows(block, rows, cols):
    pieces = [block[offset_y:offset_y + rows, offset_x:offset_x + cols] for offset_y in range(3) for offset_x in range(3)]
    return jnp.concatenate(pieces, axis=-1).reshape(rows * cols, -1)

def finish(convolved, scales):
    mean_square = lax.optimization_barrier(jnp.mean(convolved * convolved, axis=-1, keepdims=True))
    normed = convolved * lax.rsqrt(mean_square + 1e-06) * scales
    return jax.nn.silu(normed).astype(jnp.bfloat16)

def conv_layer(features, weight, scales):
    channels = features.shape[-1]
    padded = jnp.pad(features, ((2, 0), (1, 1), (1, 1), (0, 0)))
    flat_weight = weight.reshape(3, 9 * channels, channels)

    def single_frame(frame_index):
        window = lax.dynamic_slice_in_dim(padded, frame_index, 3, 0)
        accumulated = jnp.zeros((NH * NW, channels), jnp.float32)
        for offset_t in range(3):
            accumulated = accumulated + jnp.dot(tap_rows(window[offset_t], NH, NW), flat_weight[offset_t], preferred_element_type=jnp.float32)
        return accumulated
    convolved = lax.map(single_frame, jnp.arange(NF, dtype=jnp.int32))
    return finish(convolved, scales).reshape(features.shape)

def reference(frames_in, weight_first, scale_first, weight_second, scale_second):
    hidden = conv_layer(frames_in, weight_first, scale_first)
    return conv_layer(hidden, weight_second, scale_second)
```

```python
import functools

import jax
import jax.numpy as jnp
from jax import lax
from jax.experimental import pallas as pl
from jax.experimental.pallas import tpu as pltpu
from jax.sharding import PartitionSpec as P

MESH = pl.DeviceIdType.MESH
AXES = ("frame", "strip", "slab")


def exists(position, sizes, offsets):
    checks = []
    for index, size, offset in zip(position, sizes, offsets):
        if abs(offset) >= size:
            return None
        if offset > 0:
            checks.append(index < size - offset)
        elif offset < 0:
            checks.append(index >= -offset)
    return functools.reduce(jnp.logical_and, checks) if checks else True


def guarded(condition, action):
    if condition is None:
        return
    if condition is True:
        action()
    else:
        pl.when(condition)(action)


def kernel(
    sizes,
    x_ref,
    w1_hbm,
    s1_ref,
    w2_hbm,
    s2_ref,
    out_ref,
    weights,
    hidden,
    edges,
    mains,
    rows,
    tiles,
    taps,
    weight_sem,
    send_sem,
    recv_sem,
):
    frames, height, width, channels = x_ref.shape
    cells = height * width
    position = tuple(lax.axis_index(axis) for axis in AXES)

    def at(offsets):
        return {axis: index + offset for axis, index, offset in zip(AXES, position, offsets)}

    around = [(dz, ds, db) for dz in (0, 1) for ds in (-1, 0, 1) for db in (-1, 0, 1) if (dz, ds, db) != (0, 0, 0)]

    loads = []
    for layer, source in enumerate((w1_hbm, w2_hbm)):
        for offset_t in (2, 1, 0):
            copy = pltpu.make_async_copy(source.at[offset_t], weights.at[layer, offset_t], weight_sem.at[layer, offset_t])
            copy.start()
            loads.append(copy)
    loads = {(i // 3, 2 - i % 3): copy for i, copy in enumerate(loads)}

    def zero(ref, condition):
        def clear():
            ref[...] = jnp.zeros_like(ref)

        if condition is None:
            clear()
        elif condition is not True:
            pl.when(jnp.logical_not(condition))(clear)

    for layer in range(2):
        for slot in range(2 * frames):
            dz = 1 if slot < frames else 0
            if dz:
                zero(mains.at[layer, slot], exists(position, sizes, (-1, 0, 0)))
            for k, ds in ((0, 1), (1, -1)):
                zero(rows.at[layer, slot, k], exists(position, sizes, (-dz, -ds, 0)))
            for k in range(3):
                for side, db in ((0, 1), (1, -1)):
                    zero(tiles.at[layer, slot, k, side], exists(position, sizes, (-dz, k - 1, -db)))

    barrier = pltpu.get_barrier_semaphore()
    for offsets in around:
        back = tuple(-o for o in offsets)
        guarded(
            exists(position, sizes, back),
            lambda back=back: pl.semaphore_signal(barrier, inc=1, device_id=at(back), device_id_type=MESH),
        )

    def piece(layer, frame, main, offsets):
        dz, ds, db = offsets
        slot = frame if dz else frames + frame
        if db == 0 and ds == 0:
            src, dst, kind = main, mains.at[layer, slot], 0
        elif db == 0:
            row = height - 1 if ds > 0 else 0
            k = 0 if ds > 0 else 1
            src, dst, kind = main.at[row], rows.at[layer, slot, k], 1 + k
        else:
            side = 0 if db > 0 else 1
            src = edges.at[layer, frame, side]
            dst, kind = tiles.at[layer, slot, 1 - ds, side], 3 + 2 * (1 - ds) + side
        return pltpu.make_async_remote_copy(
            src_ref=src,
            dst_ref=dst,
            send_sem=send_sem.at[layer, slot, kind],
            recv_sem=recv_sem.at[layer, slot, kind],
            device_id=at(offsets),
            device_id_type=MESH,
        )

    def fill_edges(layer, frame, block):
        for side, column in ((0, width - 1), (1, 0)):
            picked = jnp.concatenate([block[r, column : column + 1] for r in range(height)], axis=0)
            edges[layer, frame, side, 0:height] = picked.astype(jnp.bfloat16)

    def send(layer, frame, main):
        order = sorted(around, key=lambda o: (-o[0], o[2] == 0, o[1] == 0))
        for offsets in order:
            guarded(exists(position, sizes, offsets), lambda o=offsets: piece(layer, frame, main, o).start())

    def receive(layer, slot, main):
        dz = 1 if slot < frames else 0
        for offsets in around:
            if offsets[0] != dz:
                continue
            back = tuple(-o for o in offsets)
            guarded(exists(position, sizes, back), lambda o=offsets: piece(layer, slot % frames, main, o).wait_recv())

    def gather(layer, slot, block_ref):
        top = rows[layer, slot, 0][None].astype(jnp.float32)
        bottom = rows[layer, slot, 1][None].astype(jnp.float32)
        block = jnp.concatenate([top, block_ref[...].astype(jnp.float32), bottom], axis=0)
        halo = []
        for side in range(2):
            above = tiles[layer, slot, 0, side].astype(jnp.float32)
            level = tiles[layer, slot, 1, side].astype(jnp.float32)
            below = tiles[layer, slot, 2, side].astype(jnp.float32)
            picked = [above[height - 1 : height]] + [level[r : r + 1] for r in range(height)] + [below[0:1]]
            halo.append(jnp.stack(picked, axis=0))
        column = lax.broadcasted_iota(jnp.int32, block.shape, 1)
        before = jnp.where(column == 0, halo[0], pltpu.roll(block, 1, 1))
        after = jnp.where(column == width - 1, halo[1], pltpu.roll(block, width - 1, 1))
        shifted = [part.astype(jnp.bfloat16) for part in (before, block, after)]
        pieces = [shifted[x][y : y + height].reshape(cells, channels) for y in range(3) for x in range(3)]
        taps[slot] = jnp.concatenate(pieces, axis=-1)

    def product(layer, slot, offset_t):
        return jnp.dot(taps[slot], weights[layer, offset_t], preferred_element_type=jnp.float32)

    def finish(convolved, scale_ref):
        mean_square = jnp.sum(convolved * convolved, axis=-1, keepdims=True) * (1.0 / channels)
        normed = convolved * lax.rsqrt(mean_square + 1e-06) * scale_ref[...]
        return (normed / (1.0 + jnp.exp(-normed))).reshape(height, width, channels)

    for frame in (1, 0):
        fill_edges(0, frame, x_ref.at[frame][...].astype(jnp.float32))

    count = jnp.int32(0)
    for offsets in around:
        condition = exists(position, sizes, offsets)
        if condition is not None:
            count = count + (1 if condition is True else condition.astype(jnp.int32))
    pl.semaphore_wait(barrier, count)

    for frame in (1, 0):
        send(0, frame, x_ref.at[frame])

    def conv_layer(layer, source, scale_ref, emit):
        for slot in (3, 2):
            receive(layer, slot, source.at[slot - 2])
            gather(layer, slot, source.at[slot - 2])
        loads[layer, 2].wait()
        late = product(layer, 3, 2)
        early = product(layer, 2, 2)
        loads[layer, 1].wait()
        late = late + product(layer, 2, 1)
        receive(layer, 1, source.at[1])
        gather(layer, 1, mains.at[layer, 1])
        loads[layer, 0].wait()
        emit(1, finish(late + product(layer, 1, 0), scale_ref))
        early = early + product(layer, 1, 1)
        receive(layer, 0, source.at[0])
        gather(layer, 0, mains.at[layer, 0])
        emit(0, finish(early + product(layer, 0, 0), scale_ref))

    def emit_hidden(frame, values):
        hidden[frame] = values.astype(jnp.bfloat16)
        fill_edges(1, frame, values)
        send(1, frame, hidden.at[frame])

    def emit_output(frame, values):
        out_ref[frame] = values.astype(jnp.bfloat16)

    conv_layer(0, x_ref, s1_ref, emit_hidden)
    conv_layer(1, hidden, s2_ref, emit_output)

    for layer, source in ((0, x_ref), (1, hidden)):
        for frame in (1, 0):
            for offsets in around:
                guarded(
                    exists(position, sizes, offsets),
                    lambda o=offsets: piece(layer, frame, source.at[frame], o).wait_send(),
                )


def shards(sizes, frames_in, weight_first, scale_first, weight_second, scale_second):
    frames, height, width, channels = frames_in.shape
    vmem, anywhere = pl.BlockSpec(memory_space=pltpu.VMEM), pl.BlockSpec(memory_space=pl.ANY)
    flat = (3, 9 * channels, channels)
    half = jnp.bfloat16
    return pl.pallas_call(
        functools.partial(kernel, sizes),
        out_shape=jax.ShapeDtypeStruct(frames_in.shape, half),
        in_specs=[vmem, anywhere, vmem, anywhere, vmem],
        out_specs=vmem,
        scratch_shapes=[
            pltpu.VMEM((2, *flat), half),
            pltpu.VMEM(frames_in.shape, half),
            pltpu.VMEM((2, frames, 2, 8, channels), half),
            pltpu.VMEM((2, frames, height, width, channels), half),
            pltpu.VMEM((2, 2 * frames, 2, width, channels), half),
            pltpu.VMEM((2, 2 * frames, 3, 2, 8, channels), half),
            pltpu.VMEM((2 * frames, height * width, 9 * channels), half),
            pltpu.SemaphoreType.DMA((2, 3)),
            pltpu.SemaphoreType.DMA((2, 2 * frames, 9)),
            pltpu.SemaphoreType.DMA((2, 2 * frames, 9)),
        ],
        compiler_params=pltpu.CompilerParams(collective_id=0, has_side_effects=True),
        name="conv_block",
    )(
        frames_in,
        weight_first.reshape(flat),
        scale_first.reshape(1, channels),
        weight_second.reshape(flat),
        scale_second.reshape(1, channels),
    )


def solution(mesh):
    sizes = tuple(mesh.shape[axis] for axis in AXES)
    return jax.shard_map(
        functools.partial(shards, sizes),
        mesh=mesh,
        in_specs=(P(("groups", "frame"), "strip", "slab", None), P(), P(), P(), P()),
        out_specs=P(("groups", "frame"), "strip", "slab", None),
        check_vma=False,
    )
```

```python
import functools

import jax
import jax.numpy as jnp
from jax import lax
from jax.experimental import pallas as pl
from jax.experimental.pallas import tpu as pltpu
from jax.sharding import PartitionSpec as P

MESH = pl.DeviceIdType.MESH
AXES = ("frame", "strip", "slab")


def exists(position, sizes, offsets):
    checks = []
    for index, size, offset in zip(position, sizes, offsets):
        if abs(offset) >= size:
            return None
        if offset > 0:
            checks.append(index < size - offset)
        elif offset < 0:
            checks.append(index >= -offset)
    return functools.reduce(jnp.logical_and, checks) if checks else True


def guarded(condition, action):
    if condition is None:
        return
    if condition is True:
        action()
    else:
        pl.when(condition)(action)


def pack(block):
    lead, half = 128, block.shape[1] // 2
    rest = block[..., lead:]
    return jnp.concatenate([block[..., :lead], jnp.concatenate([rest[:, :half], rest[:, half:]], axis=-1)], axis=1)


def unpack(packed, width):
    rest, lanes = packed[:, width:], packed.shape[-1] // 2
    rest = jnp.concatenate([rest[..., :lanes], rest[..., lanes:]], axis=1)
    return jnp.concatenate([packed[:, :width], rest], axis=-1)


def kernel(
    sizes,
    x_hbm,
    w1_hbm,
    s1_hbm,
    w2_hbm,
    s2_hbm,
    out_ref,
    x_ref,
    scales,
    staged,
    weights,
    packs,
    edges,
    mains,
    rows,
    tiles,
    taps,
    local_sem,
    weight_sem,
    send_sem,
    recv_sem,
):
    frames, height, width, channels = x_ref.shape
    cells = height * width
    position = tuple(lax.axis_index(axis) for axis in AXES)

    def at(offsets):
        return {axis: index + offset for axis, index, offset in zip(AXES, position, offsets)}

    around = [(dz, ds, db) for dz in (0, 1) for ds in (-1, 0, 1) for db in (-1, 0, 1) if (dz, ds, db) != (0, 0, 0)]

    barrier = pltpu.get_barrier_semaphore()
    for offsets in around:
        back = tuple(-o for o in offsets)
        guarded(
            exists(position, sizes, back),
            lambda back=back: pl.semaphore_signal(barrier, inc=1, device_id=at(back), device_id_type=MESH),
        )

    x_loads = [pltpu.make_async_copy(x_hbm.at[frame], x_ref.at[frame], local_sem.at[frame]) for frame in range(2)]
    for frame in (1, 0):
        x_loads[frame].start()

    loads = []
    for layer, source in enumerate((w1_hbm, w2_hbm)):
        for offset_t in (2, 1, 0):
            copy = pltpu.make_async_copy(source.at[offset_t], weights.at[layer, offset_t], weight_sem.at[layer, offset_t])
            copy.start()
            loads.append(copy)
    loads = {(i // 3, 2 - i % 3): copy for i, copy in enumerate(loads)}
    scale_loads = [pltpu.make_async_copy(ref, scales.at[layer], local_sem.at[2 + layer]) for layer, ref in enumerate((s1_hbm, s2_hbm))]
    for copy in scale_loads:
        copy.start()
    out_copies = [pltpu.make_async_copy(staged.at[frame], out_ref.at[frame], local_sem.at[4 + frame]) for frame in range(2)]

    def piece(layer, frame, main, offsets):
        dz, ds, db = offsets
        slot = frame if dz else frames + frame
        if db == 0 and ds == 0:
            src, dst, kind = main, mains.at[layer, slot], 0
        elif db == 0:
            row = height - 1 if ds > 0 else 0
            k = 0 if ds > 0 else 1
            src, dst, kind = main.at[row], rows.at[layer, slot, k], 1 + k
        else:
            side = 0 if db > 0 else 1
            src = edges.at[layer, frame, side]
            dst, kind = tiles.at[layer, slot, 1 - ds, side], 3 + 2 * (1 - ds) + side
        return pltpu.make_async_remote_copy(
            src_ref=src,
            dst_ref=dst,
            send_sem=send_sem.at[layer, slot, kind],
            recv_sem=recv_sem.at[layer, slot, kind],
            device_id=at(offsets),
            device_id_type=MESH,
        )

    def fill_edges(layer, frame, block):
        for side, column in ((0, width - 1), (1, 0)):
            picked = jnp.concatenate([block[r, column : column + 1] for r in range(height)], axis=0)
            edges[layer, frame, side, 0:height] = picked.astype(jnp.bfloat16)

    def send(layer, frame, main):
        order = sorted(around, key=lambda o: (o[0], o[2] == 0, o[1] == 0))
        for offsets in order:
            guarded(exists(position, sizes, offsets), lambda o=offsets: piece(layer, frame, main, o).start())

    def receive(layer, slot, main):
        dz = 1 if slot < frames else 0
        for offsets in around:
            if offsets[0] != dz:
                continue
            back = tuple(-o for o in offsets)
            guarded(exists(position, sizes, back), lambda o=offsets: piece(layer, slot % frames, main, o).wait_recv())

    def gather(layer, slot, block_ref):
        block = jnp.concatenate([rows[layer, slot, 0][None], block_ref[...], rows[layer, slot, 1][None]], axis=0)
        block = unpack(block, width).astype(jnp.float32)
        halo = []
        for side in range(2):
            above = tiles[layer, slot, 0, side].astype(jnp.float32)
            level = tiles[layer, slot, 1, side].astype(jnp.float32)
            below = tiles[layer, slot, 2, side].astype(jnp.float32)
            picked = [above[height - 1 : height]] + [level[r : r + 1] for r in range(height)] + [below[0:1]]
            halo.append(jnp.stack(picked, axis=0))
        column = lax.broadcasted_iota(jnp.int32, block.shape, 1)
        before = jnp.where(column == 0, halo[0], pltpu.roll(block, 1, 1))
        after = jnp.where(column == width - 1, halo[1], pltpu.roll(block, width - 1, 1))
        shifted = [part.astype(jnp.bfloat16) for part in (before, block, after)]
        pieces = [shifted[x][y : y + height].reshape(cells, channels) for y in range(3) for x in range(3)]
        taps[slot] = jnp.concatenate(pieces, axis=-1)

    def product(layer, slot, offset_t):
        return jnp.dot(taps[slot], weights[layer, offset_t], preferred_element_type=jnp.float32)

    def finish(convolved, layer):
        mean_square = jnp.sum(convolved * convolved, axis=-1, keepdims=True) * (1.0 / channels)
        normed = convolved * lax.rsqrt(mean_square + 1e-06) * scales[layer]
        return (normed / (1.0 + jnp.exp(-normed))).reshape(height, width, channels)

    for frame in (1, 0):
        x_loads[frame].wait()
        packs[0, frame] = pack(x_ref[frame])
        fill_edges(0, frame, x_ref[frame].astype(jnp.float32))

    count = jnp.int32(0)
    for offsets in around:
        condition = exists(position, sizes, offsets)
        if condition is not None:
            count = count + (1 if condition is True else condition.astype(jnp.int32))
    pl.semaphore_wait(barrier, count)

    for frame in (1, 0):
        send(0, frame, packs.at[0, frame])

    def zero(ref, condition):
        def clear():
            ref[...] = jnp.zeros_like(ref)

        if condition is None:
            clear()
        elif condition is not True:
            pl.when(jnp.logical_not(condition))(clear)

    for layer in range(2):
        for slot in range(2 * frames):
            dz = 1 if slot < frames else 0
            if dz:
                zero(mains.at[layer, slot], exists(position, sizes, (-1, 0, 0)))
            for k, ds in ((0, 1), (1, -1)):
                zero(rows.at[layer, slot, k], exists(position, sizes, (-dz, -ds, 0)))
            for k in range(3):
                for side, db in ((0, 1), (1, -1)):
                    zero(tiles.at[layer, slot, k, side], exists(position, sizes, (-dz, k - 1, -db)))
    for copy in scale_loads:
        copy.wait()

    def conv_layer(layer, source, emit):
        for slot in (3, 2):
            receive(layer, slot, source.at[slot - 2])
            gather(layer, slot, source.at[slot - 2])
        loads[layer, 2].wait()
        late = product(layer, 3, 2)
        early = product(layer, 2, 2)
        loads[layer, 1].wait()
        late = late + product(layer, 2, 1)
        receive(layer, 1, source.at[1])
        gather(layer, 1, mains.at[layer, 1])
        loads[layer, 0].wait()
        emit(1, finish(late + product(layer, 1, 0), layer))
        early = early + product(layer, 1, 1)
        receive(layer, 0, source.at[0])
        gather(layer, 0, mains.at[layer, 0])
        emit(0, finish(early + product(layer, 0, 0), layer))

    def emit_hidden(frame, values):
        packs[1, frame] = pack(values).astype(jnp.bfloat16)
        fill_edges(1, frame, values)
        send(1, frame, packs.at[1, frame])

    def emit_output(frame, values):
        staged[frame] = values.astype(jnp.bfloat16)
        out_copies[frame].start()

    conv_layer(0, packs.at[0], emit_hidden)
    conv_layer(1, packs.at[1], emit_output)

    for layer in range(2):
        for frame in (1, 0):
            for offsets in around:
                guarded(
                    exists(position, sizes, offsets),
                    lambda o=offsets: piece(layer, frame, packs.at[layer, frame], o).wait_send(),
                )
    for copy in out_copies:
        copy.wait()


def shards(sizes, frames_in, weight_first, scale_first, weight_second, scale_second):
    frames, height, width, channels = frames_in.shape
    anywhere = pl.BlockSpec(memory_space=pl.ANY)
    lines = width * channels // 128
    flat = (3, 9 * channels, channels)
    half = jnp.bfloat16
    return pl.pallas_call(
        functools.partial(kernel, sizes),
        out_shape=jax.ShapeDtypeStruct(frames_in.shape, half),
        in_specs=[anywhere] * 5,
        out_specs=anywhere,
        scratch_shapes=[
            pltpu.VMEM(frames_in.shape, half),
            pltpu.VMEM((2, 1, channels), jnp.float32),
            pltpu.VMEM(frames_in.shape, half),
            pltpu.VMEM((2, *flat), half),
            pltpu.VMEM((2, frames, height, lines, 128), half),
            pltpu.VMEM((2, frames, 2, 8, channels), half),
            pltpu.VMEM((2, frames, height, lines, 128), half),
            pltpu.VMEM((2, 2 * frames, 2, lines, 128), half),
            pltpu.VMEM((2, 2 * frames, 3, 2, 8, channels), half),
            pltpu.VMEM((2 * frames, height * width, 9 * channels), half),
            pltpu.SemaphoreType.DMA((6,)),
            pltpu.SemaphoreType.DMA((2, 3)),
            pltpu.SemaphoreType.DMA((2, 2 * frames, 9)),
            pltpu.SemaphoreType.DMA((2, 2 * frames, 9)),
        ],
        compiler_params=pltpu.CompilerParams(collective_id=0, has_side_effects=True),
        name="conv_block",
    )(
        frames_in,
        weight_first.reshape(flat),
        scale_first.reshape(1, channels),
        weight_second.reshape(flat),
        scale_second.reshape(1, channels),
    )


def solution(mesh):
    sizes = tuple(mesh.shape[axis] for axis in AXES)
    return jax.shard_map(
        functools.partial(shards, sizes),
        mesh=mesh,
        in_specs=(P(("groups", "frame"), "strip", "slab", None), P(), P(), P(), P()),
        out_specs=P(("groups", "frame"), "strip", "slab", None),
        check_vma=False,
    )
```

```python
import functools

import jax
import jax.numpy as jnp
from jax import lax
from jax.experimental import pallas as pl
from jax.experimental.pallas import tpu as pltpu
from jax.sharding import PartitionSpec as P

MESH = pl.DeviceIdType.MESH
AXES = ("frame", "strip", "slab")


def exists(position, sizes, offsets):
    checks = []
    for index, size, offset in zip(position, sizes, offsets):
        if abs(offset) >= size:
            return None
        if offset > 0:
            checks.append(index < size - offset)
        elif offset < 0:
            checks.append(index >= -offset)
    return functools.reduce(jnp.logical_and, checks) if checks else True


def guarded(condition, action):
    if condition is None:
        return
    if condition is True:
        action()
    else:
        pl.when(condition)(action)


def pack(block):
    lead, half = 128, block.shape[1] // 2
    rest = block[..., lead:]
    return jnp.concatenate([block[..., :lead], jnp.concatenate([rest[:, :half], rest[:, half:]], axis=-1)], axis=1)


def unpack(packed, width):
    rest, lanes = packed[:, width:], packed.shape[-1] // 2
    rest = jnp.concatenate([rest[..., :lanes], rest[..., lanes:]], axis=1)
    return jnp.concatenate([packed[:, :width], rest], axis=-1)


def kernel(
    sizes,
    x_hbm,
    w1_hbm,
    s1_hbm,
    w2_hbm,
    s2_hbm,
    out_ref,
    x_ref,
    scales,
    weights,
    packs,
    edges,
    mains,
    rows,
    tiles,
    taps,
    local_sem,
    weight_sem,
    send_sem,
    recv_sem,
):
    frames, height, width, channels = x_ref.shape
    cells = height * width
    position = tuple(lax.axis_index(axis) for axis in AXES)

    def at(offsets):
        return {axis: index + offset for axis, index, offset in zip(AXES, position, offsets)}

    around = [(dz, ds, db) for dz in (0, 1) for ds in (-1, 0, 1) for db in (-1, 0, 1)]
    around = [o for o in around if o != (0, 0, 0) and (o[0] == 0 or o[1] == 0 or o[2] != 0)]

    barrier = pltpu.get_barrier_semaphore()
    for offsets in around:
        back = tuple(-o for o in offsets)
        guarded(
            exists(position, sizes, back),
            lambda back=back: pl.semaphore_signal(barrier, inc=1, device_id=at(back), device_id_type=MESH),
        )

    x_loads = [pltpu.make_async_copy(x_hbm.at[frame], x_ref.at[frame], local_sem.at[frame]) for frame in range(2)]
    for frame in (1, 0):
        x_loads[frame].start()

    loads = []
    for layer, source in enumerate((w1_hbm, w2_hbm)):
        for offset_t in (2, 1, 0):
            copy = pltpu.make_async_copy(source.at[offset_t], weights.at[layer, offset_t], weight_sem.at[layer, offset_t])
            copy.start()
            loads.append(copy)
    loads = {(i // 3, 2 - i % 3): copy for i, copy in enumerate(loads)}
    scale_loads = [pltpu.make_async_copy(ref, scales.at[layer], local_sem.at[2 + layer]) for layer, ref in enumerate((s1_hbm, s2_hbm))]
    for copy in scale_loads:
        copy.start()

    def piece(layer, frame, main, offsets):
        dz, ds, db = offsets
        slot = frame if dz else frames + frame
        if db == 0 and ds == 0:
            part = pl.ds(1, height - 2)
            src, dst, kind = main.at[part], mains.at[layer, slot, part], 0
        elif db == 0:
            row = height - 1 if ds > 0 else 0
            k = 0 if ds > 0 else 1
            src, dst, kind = main.at[row], rows.at[layer, slot, k], 1 + k
        else:
            side = 0 if db > 0 else 1
            src = edges.at[layer, frame, side]
            dst, kind = tiles.at[layer, slot, 1 - ds, side], 3 + 2 * (1 - ds) + side
        return pltpu.make_async_remote_copy(
            src_ref=src,
            dst_ref=dst,
            send_sem=send_sem.at[layer, slot, kind],
            recv_sem=recv_sem.at[layer, slot, kind],
            device_id=at(offsets),
            device_id_type=MESH,
        )

    def fill_edges(layer, frame, block):
        for side, column in ((0, width - 1), (1, 0)):
            picked = jnp.concatenate([block[r, column : column + 1] for r in range(height)], axis=0)
            edges[layer, frame, side, 0:height] = picked.astype(jnp.bfloat16)

    behind, ahead = exists(position, sizes, (-1, 0, 0)), exists(position, sizes, (1, 0, 0))

    def both(first, second):
        if first is None or second is None:
            return None
        return jnp.logical_and(first, second)

    def edge_row(layer, frame, ds):
        row, kind = (height - 1, 10) if ds > 0 else (0, 9)
        return pltpu.make_async_remote_copy(
            src_ref=packs.at[layer, frame, row],
            dst_ref=mains.at[layer, frame, row],
            send_sem=send_sem.at[layer, frame, kind],
            recv_sem=recv_sem.at[layer, frame, kind],
            device_id=at((1, 0, 0)),
            device_id_type=MESH,
        )

    def passed_on(layer, frame, ds):
        row, k = (height - 1, 0) if ds > 0 else (0, 1)
        return pltpu.make_async_remote_copy(
            src_ref=mains.at[layer, frame, row],
            dst_ref=rows.at[layer, frame, k],
            send_sem=send_sem.at[layer, frame, 1 + k],
            recv_sem=recv_sem.at[layer, frame, 1 + k],
            device_id=at((0, ds, 0)),
            device_id_type=MESH,
        )

    def beside(ds):
        has = exists(position, sizes, (0, ds, 0))
        return (None, True) if has is None else (has, jnp.logical_not(has))

    def send_edges(layer, frame, main):
        for offsets in around:
            if offsets[0] == 0:
                guarded(exists(position, sizes, offsets), lambda o=offsets: piece(layer, frame, main, o).start())
        for ds in (1, -1):
            guarded(both(ahead, beside(ds)[0]), lambda ds=ds: edge_row(layer, frame, ds).start())

    def send_rest(layer, frame, main):
        for offsets in around:
            if offsets[0] == 1 and offsets[2] != 0:
                guarded(exists(position, sizes, offsets), lambda o=offsets: piece(layer, frame, main, o).start())
        guarded(ahead, lambda: piece(layer, frame, main, (1, 0, 0)).start())
        for ds in (1, -1):
            guarded(both(ahead, beside(ds)[1]), lambda ds=ds: edge_row(layer, frame, ds).start())

    def pass_on(layer, frame):
        for ds in (1, -1):

            def act(ds=ds):
                edge_row(layer, frame, ds).wait_recv()
                passed_on(layer, frame, ds).start()

            guarded(both(behind, beside(ds)[0]), act)

    def receive(layer, slot, main):
        dz = 1 if slot < frames else 0
        for offsets in around:
            if offsets[0] != dz:
                continue
            back = tuple(-o for o in offsets)
            guarded(exists(position, sizes, back), lambda o=offsets: piece(layer, slot % frames, main, o).wait_recv())
        if dz:
            for ds in (1, -1):
                guarded(both(behind, beside(ds)[1]), lambda ds=ds: edge_row(layer, slot, ds).wait_recv())
                guarded(both(behind, beside(-ds)[0]), lambda ds=ds: passed_on(layer, slot, ds).wait_recv())

    def gather(layer, slot, block_ref):
        block = jnp.concatenate([rows[layer, slot, 0][None], block_ref[...], rows[layer, slot, 1][None]], axis=0)
        block = unpack(block, width).astype(jnp.float32)
        halo = []
        for side in range(2):
            above = tiles[layer, slot, 0, side].astype(jnp.float32)
            level = tiles[layer, slot, 1, side].astype(jnp.float32)
            below = tiles[layer, slot, 2, side].astype(jnp.float32)
            picked = [above[height - 1 : height]] + [level[r : r + 1] for r in range(height)] + [below[0:1]]
            halo.append(jnp.stack(picked, axis=0))
        column = lax.broadcasted_iota(jnp.int32, block.shape, 1)
        before = jnp.where(column == 0, halo[0], pltpu.roll(block, 1, 1))
        after = jnp.where(column == width - 1, halo[1], pltpu.roll(block, width - 1, 1))
        shifted = [part.astype(jnp.bfloat16) for part in (before, block, after)]
        pieces = [shifted[x][y : y + height].reshape(cells, channels) for y in range(3) for x in range(3)]
        taps[slot] = jnp.concatenate(pieces, axis=-1)

    def product(layer, slot, offset_t):
        return jnp.dot(taps[slot], weights[layer, offset_t], preferred_element_type=jnp.float32)

    def finish(convolved, layer):
        mean_square = jnp.sum(convolved * convolved, axis=-1, keepdims=True) * (1.0 / channels)
        normed = convolved * lax.rsqrt(mean_square + 1e-06) * scales[layer]
        return (normed / (1.0 + jnp.exp(-normed))).reshape(height, width, channels)

    for frame in (1, 0):
        x_loads[frame].wait()
        packs[0, frame] = pack(x_ref[frame])
        fill_edges(0, frame, x_ref[frame].astype(jnp.float32))

    count = jnp.int32(0)
    for offsets in around:
        condition = exists(position, sizes, offsets)
        if condition is not None:
            count = count + (1 if condition is True else condition.astype(jnp.int32))
    pl.semaphore_wait(barrier, count)

    for frame in (1, 0):
        send_edges(0, frame, packs.at[0, frame])
    for frame in (1, 0):
        send_rest(0, frame, packs.at[0, frame])

    def zero(ref, condition):
        def clear():
            ref[...] = jnp.zeros_like(ref)

        if condition is None:
            clear()
        elif condition is not True:
            pl.when(jnp.logical_not(condition))(clear)

    for layer in range(2):
        for slot in range(2 * frames):
            dz = 1 if slot < frames else 0
            if dz:
                zero(mains.at[layer, slot], exists(position, sizes, (-1, 0, 0)))
            for k, ds in ((0, 1), (1, -1)):
                zero(rows.at[layer, slot, k], exists(position, sizes, (-dz, -ds, 0)))
            for k in range(3):
                for side, db in ((0, 1), (1, -1)):
                    zero(tiles.at[layer, slot, k, side], exists(position, sizes, (-dz, k - 1, -db)))
    for copy in scale_loads:
        copy.wait()

    def conv_layer(layer, source, emit):
        for slot in (3, 2):
            receive(layer, slot, source.at[slot - 2])
            gather(layer, slot, source.at[slot - 2])
        pass_on(layer, 1)
        if layer == 0:
            pass_on(layer, 0)
        loads[layer, 2].wait()
        late = product(layer, 3, 2)
        early = product(layer, 2, 2)
        loads[layer, 1].wait()
        late = late + product(layer, 2, 1)
        receive(layer, 1, source.at[1])
        gather(layer, 1, mains.at[layer, 1])
        if layer == 1:
            pass_on(layer, 0)
        loads[layer, 0].wait()
        emit(1, finish(late + product(layer, 1, 0), layer))
        early = early + product(layer, 1, 1)
        receive(layer, 0, source.at[0])
        gather(layer, 0, mains.at[layer, 0])
        emit(0, finish(early + product(layer, 0, 0), layer))

    def emit_hidden(frame, values):
        packs[1, frame] = pack(values).astype(jnp.bfloat16)
        fill_edges(1, frame, values)
        send_edges(1, frame, packs.at[1, frame])
        send_rest(1, frame, packs.at[1, frame])

    def emit_output(frame, values):
        out_ref[frame] = values.astype(jnp.bfloat16)

    conv_layer(0, packs.at[0], emit_hidden)
    conv_layer(1, packs.at[1], emit_output)

    for layer in range(2):
        for frame in (1, 0):
            for offsets in around:
                guarded(
                    exists(position, sizes, offsets),
                    lambda o=offsets: piece(layer, frame, packs.at[layer, frame], o).wait_send(),
                )
            for ds in (1, -1):
                guarded(ahead, lambda ds=ds: edge_row(layer, frame, ds).wait_send())
                guarded(both(behind, beside(ds)[0]), lambda ds=ds: passed_on(layer, frame, ds).wait_send())


def shards(sizes, frames_in, weight_first, scale_first, weight_second, scale_second):
    frames, height, width, channels = frames_in.shape
    anywhere = pl.BlockSpec(memory_space=pl.ANY)
    lines = width * channels // 128
    flat = (3, 9 * channels, channels)
    half = jnp.bfloat16
    return pl.pallas_call(
        functools.partial(kernel, sizes),
        out_shape=pltpu.VMEM(frames_in.shape, half),
        in_specs=[anywhere] * 5,
        out_specs=pl.BlockSpec(memory_space=pltpu.VMEM),
        scratch_shapes=[
            pltpu.VMEM(frames_in.shape, half),
            pltpu.VMEM((2, 1, channels), jnp.float32),
            pltpu.VMEM((2, *flat), half),
            pltpu.VMEM((2, frames, height, lines, 128), half),
            pltpu.VMEM((2, frames, 2, 8, channels), half),
            pltpu.VMEM((2, frames, height, lines, 128), half),
            pltpu.VMEM((2, 2 * frames, 2, lines, 128), half),
            pltpu.VMEM((2, 2 * frames, 3, 2, 8, channels), half),
            pltpu.VMEM((2 * frames, height * width, 9 * channels), half),
            pltpu.SemaphoreType.DMA((4,)),
            pltpu.SemaphoreType.DMA((2, 3)),
            pltpu.SemaphoreType.DMA((2, 2 * frames, 11)),
            pltpu.SemaphoreType.DMA((2, 2 * frames, 11)),
        ],
        compiler_params=pltpu.CompilerParams(collective_id=0, has_side_effects=True),
        name="conv_block",
    )(
        frames_in,
        weight_first.reshape(flat),
        scale_first.reshape(1, channels),
        weight_second.reshape(flat),
        scale_second.reshape(1, channels),
    )


def solution(mesh):
    sizes = tuple(mesh.shape[axis] for axis in AXES)
    return jax.shard_map(
        functools.partial(shards, sizes),
        mesh=mesh,
        in_specs=(P(("groups", "frame"), "strip", "slab", None), P(), P(), P(), P()),
        out_specs=P(("groups", "frame"), "strip", "slab", None),
        check_vma=False,
    )
```

```python
import functools

import jax
import jax.numpy as jnp
from jax import lax
from jax.experimental import pallas as pl
from jax.experimental.pallas import tpu as pltpu
from jax.sharding import PartitionSpec as P

MESH = pl.DeviceIdType.MESH
AXES = ("frame", "strip", "slab")


def exists(position, sizes, offsets):
    checks = []
    for index, size, offset in zip(position, sizes, offsets):
        if abs(offset) >= size:
            return None
        if offset > 0:
            checks.append(index < size - offset)
        elif offset < 0:
            checks.append(index >= -offset)
    return functools.reduce(jnp.logical_and, checks) if checks else True


def guarded(condition, action):
    if condition is None:
        return
    if condition is True:
        action()
    else:
        pl.when(condition)(action)


def pack(block):
    lead, half = 128, block.shape[1] // 2
    rest = block[..., lead:]
    return jnp.concatenate([block[..., :lead], jnp.concatenate([rest[:, :half], rest[:, half:]], axis=-1)], axis=1)


def unpack(packed, width):
    rest, lanes = packed[:, width:], packed.shape[-1] // 2
    rest = jnp.concatenate([rest[..., :lanes], rest[..., lanes:]], axis=1)
    return jnp.concatenate([packed[:, :width], rest], axis=-1)


def kernel(
    sizes,
    x_hbm,
    w1_hbm,
    s1_hbm,
    w2_hbm,
    s2_hbm,
    out_ref,
    x_ref,
    scales,
    weights,
    packs,
    edges,
    mains,
    rows,
    tiles,
    taps,
    local_sem,
    weight_sem,
    send_sem,
    recv_sem,
):
    frames, height, width, channels = x_ref.shape
    cells = height * width
    position = tuple(lax.axis_index(axis) for axis in AXES)

    def at(offsets):
        return {axis: index + offset for axis, index, offset in zip(AXES, position, offsets)}

    around = [(dz, ds, db) for dz in (0, 1) for ds in (-1, 0, 1) for db in (-1, 0, 1) if (dz, ds, db) != (0, 0, 0)]

    barrier = pltpu.get_barrier_semaphore()
    for offsets in around:
        back = tuple(-o for o in offsets)
        guarded(
            exists(position, sizes, back),
            lambda back=back: pl.semaphore_signal(barrier, inc=1, device_id=at(back), device_id_type=MESH),
        )

    x_loads = [pltpu.make_async_copy(x_hbm.at[frame], x_ref.at[frame], local_sem.at[frame]) for frame in range(2)]
    for frame in (1, 0):
        x_loads[frame].start()

    loads = []
    for layer, source in enumerate((w1_hbm, w2_hbm)):
        for offset_t in (2, 1, 0):
            copy = pltpu.make_async_copy(source.at[offset_t], weights.at[layer, offset_t], weight_sem.at[layer, offset_t])
            copy.start()
            loads.append(copy)
    loads = {(i // 3, 2 - i % 3): copy for i, copy in enumerate(loads)}
    scale_loads = [pltpu.make_async_copy(ref, scales.at[layer], local_sem.at[2 + layer]) for layer, ref in enumerate((s1_hbm, s2_hbm))]
    for copy in scale_loads:
        copy.start()

    def piece(layer, frame, main, offsets):
        dz, ds, db = offsets
        slot = frame if dz else frames + frame
        if db == 0 and ds == 0:
            src, dst, kind = main, mains.at[layer, slot], 0
        elif db == 0:
            row = height - 1 if ds > 0 else 0
            k = 0 if ds > 0 else 1
            src, dst, kind = main.at[row], rows.at[layer, slot, k], 1 + k
        else:
            side = 0 if db > 0 else 1
            src = edges.at[layer, frame, side]
            dst, kind = tiles.at[layer, slot, 1 - ds, side], 3 + 2 * (1 - ds) + side
        return pltpu.make_async_remote_copy(
            src_ref=src,
            dst_ref=dst,
            send_sem=send_sem.at[layer, slot, kind],
            recv_sem=recv_sem.at[layer, slot, kind],
            device_id=at(offsets),
            device_id_type=MESH,
        )

    def fill_edges(layer, frame, block):
        for side, column in ((0, width - 1), (1, 0)):
            picked = jnp.concatenate([block[r, column : column + 1] for r in range(height)], axis=0)
            edges[layer, frame, side, 0:height] = picked.astype(jnp.bfloat16)

    def send(layer, frame, main):
        order = sorted(around, key=lambda o: (o[0], o[2] == 0, o[1] == 0))
        for offsets in order:
            guarded(exists(position, sizes, offsets), lambda o=offsets: piece(layer, frame, main, o).start())

    def receive(layer, slot, main):
        dz = 1 if slot < frames else 0
        for offsets in around:
            if offsets[0] != dz:
                continue
            back = tuple(-o for o in offsets)
            guarded(exists(position, sizes, back), lambda o=offsets: piece(layer, slot % frames, main, o).wait_recv())

    def gather(layer, slot, block_ref):
        block = jnp.concatenate([rows[layer, slot, 0][None], block_ref[...], rows[layer, slot, 1][None]], axis=0)
        block = unpack(block, width).astype(jnp.float32)
        halo = []
        for side in range(2):
            above = tiles[layer, slot, 0, side].astype(jnp.float32)
            level = tiles[layer, slot, 1, side].astype(jnp.float32)
            below = tiles[layer, slot, 2, side].astype(jnp.float32)
            picked = [above[height - 1 : height]] + [level[r : r + 1] for r in range(height)] + [below[0:1]]
            halo.append(jnp.stack(picked, axis=0))
        column = lax.broadcasted_iota(jnp.int32, block.shape, 1)
        before = jnp.where(column == 0, halo[0], pltpu.roll(block, 1, 1))
        after = jnp.where(column == width - 1, halo[1], pltpu.roll(block, width - 1, 1))
        shifted = [part.astype(jnp.bfloat16) for part in (before, block, after)]
        pieces = [shifted[x][y : y + height].reshape(cells, channels) for y in range(3) for x in range(3)]
        taps[slot] = jnp.concatenate(pieces, axis=-1)

    def product(layer, slot, offset_t):
        return jnp.dot(taps[slot], weights[layer, offset_t], preferred_element_type=jnp.float32)

    def finish(convolved, layer):
        mean_square = jnp.sum(convolved * convolved, axis=-1, keepdims=True) * (1.0 / channels)
        normed = convolved * lax.rsqrt(mean_square + 1e-06) * scales[layer]
        return (normed / (1.0 + jnp.exp(-normed))).reshape(height, width, channels)

    for frame in (1, 0):
        x_loads[frame].wait()
        packs[0, frame] = pack(x_ref[frame])
        fill_edges(0, frame, x_ref[frame].astype(jnp.float32))

    count = jnp.int32(0)
    for offsets in around:
        condition = exists(position, sizes, offsets)
        if condition is not None:
            count = count + (1 if condition is True else condition.astype(jnp.int32))
    pl.semaphore_wait(barrier, count)

    for frame in (1, 0):
        send(0, frame, packs.at[0, frame])

    def zero(ref, condition):
        def clear():
            ref[...] = jnp.zeros_like(ref)

        if condition is None:
            clear()
        elif condition is not True:
            pl.when(jnp.logical_not(condition))(clear)

    for layer in range(2):
        for slot in range(2 * frames):
            dz = 1 if slot < frames else 0
            if dz:
                zero(mains.at[layer, slot], exists(position, sizes, (-1, 0, 0)))
            for k, ds in ((0, 1), (1, -1)):
                zero(rows.at[layer, slot, k], exists(position, sizes, (-dz, -ds, 0)))
            for k in range(3):
                for side, db in ((0, 1), (1, -1)):
                    zero(tiles.at[layer, slot, k, side], exists(position, sizes, (-dz, k - 1, -db)))
    for copy in scale_loads:
        copy.wait()

    def conv_layer(layer, source, emit):
        receive(layer, 3, source.at[1])
        gather(layer, 3, source.at[1])
        loads[layer, 2].wait()
        late = product(layer, 3, 2)
        receive(layer, 2, source.at[0])
        gather(layer, 2, source.at[0])
        early = product(layer, 2, 2)
        loads[layer, 1].wait()
        late = late + product(layer, 2, 1)
        receive(layer, 1, source.at[1])
        gather(layer, 1, mains.at[layer, 1])
        loads[layer, 0].wait()
        emit(1, finish(late + product(layer, 1, 0), layer))
        early = early + product(layer, 1, 1)
        receive(layer, 0, source.at[0])
        gather(layer, 0, mains.at[layer, 0])
        emit(0, finish(early + product(layer, 0, 0), layer))

    def emit_hidden(frame, values):
        packs[1, frame] = pack(values).astype(jnp.bfloat16)
        fill_edges(1, frame, values)
        send(1, frame, packs.at[1, frame])

    def emit_output(frame, values):
        out_ref[frame] = values.astype(jnp.bfloat16)

    conv_layer(0, packs.at[0], emit_hidden)
    conv_layer(1, packs.at[1], emit_output)

    for layer in range(2):
        for frame in (1, 0):
            for offsets in around:
                guarded(
                    exists(position, sizes, offsets),
                    lambda o=offsets: piece(layer, frame, packs.at[layer, frame], o).wait_send(),
                )


def shards(sizes, frames_in, weight_first, scale_first, weight_second, scale_second):
    frames, height, width, channels = frames_in.shape
    anywhere = pl.BlockSpec(memory_space=pl.ANY)
    lines = width * channels // 128
    flat = (3, 9 * channels, channels)
    half = jnp.bfloat16
    return pl.pallas_call(
        functools.partial(kernel, sizes),
        out_shape=pltpu.VMEM(frames_in.shape, half),
        in_specs=[anywhere] * 5,
        out_specs=pl.BlockSpec(memory_space=pltpu.VMEM),
        scratch_shapes=[
            pltpu.VMEM(frames_in.shape, half),
            pltpu.VMEM((2, 1, channels), jnp.float32),
            pltpu.VMEM((2, *flat), half),
            pltpu.VMEM((2, frames, height, lines, 128), half),
            pltpu.VMEM((2, frames, 2, 8, channels), half),
            pltpu.VMEM((2, frames, height, lines, 128), half),
            pltpu.VMEM((2, 2 * frames, 2, lines, 128), half),
            pltpu.VMEM((2, 2 * frames, 3, 2, 8, channels), half),
            pltpu.VMEM((2 * frames, height * width, 9 * channels), half),
            pltpu.SemaphoreType.DMA((4,)),
            pltpu.SemaphoreType.DMA((2, 3)),
            pltpu.SemaphoreType.DMA((2, 2 * frames, 9)),
            pltpu.SemaphoreType.DMA((2, 2 * frames, 9)),
        ],
        compiler_params=pltpu.CompilerParams(collective_id=0, has_side_effects=True),
        name="conv_block",
    )(
        frames_in,
        weight_first.reshape(flat),
        scale_first.reshape(1, channels),
        weight_second.reshape(flat),
        scale_second.reshape(1, channels),
    )


def solution(mesh):
    sizes = tuple(mesh.shape[axis] for axis in AXES)
    return jax.shard_map(
        functools.partial(shards, sizes),
        mesh=mesh,
        in_specs=(P(("groups", "frame"), "strip", "slab", None), P(), P(), P(), P()),
        out_specs=P(("groups", "frame"), "strip", "slab", None),
        check_vma=False,
    )
```

```python
import functools

import jax
import jax.numpy as jnp
from jax import lax
from jax.experimental import pallas as pl
from jax.experimental.pallas import tpu as pltpu
from jax.sharding import PartitionSpec as P

MESH = pl.DeviceIdType.MESH
AXES = ("frame", "strip", "slab")


def exists(position, sizes, offsets):
    checks = []
    for index, size, offset in zip(position, sizes, offsets):
        if abs(offset) >= size:
            return None
        if offset > 0:
            checks.append(index < size - offset)
        elif offset < 0:
            checks.append(index >= -offset)
    return functools.reduce(jnp.logical_and, checks) if checks else True


def guarded(condition, action):
    if condition is None:
        return
    if condition is True:
        action()
    else:
        pl.when(condition)(action)


def pack(block):
    lead, half = 128, block.shape[1] // 2
    rest = block[..., lead:]
    return jnp.concatenate([block[..., :lead], jnp.concatenate([rest[:, :half], rest[:, half:]], axis=-1)], axis=1)


def unpack(packed, width):
    rest, lanes = packed[:, width:], packed.shape[-1] // 2
    rest = jnp.concatenate([rest[..., :lanes], rest[..., lanes:]], axis=1)
    return jnp.concatenate([packed[:, :width], rest], axis=-1)


def kernel(
    sizes,
    x_hbm,
    w1_hbm,
    s1_hbm,
    w2_hbm,
    s2_hbm,
    out_ref,
    x_ref,
    scales,
    weights,
    packs,
    edges,
    mains,
    rows,
    tiles,
    taps,
    local_sem,
    weight_sem,
    send_sem,
    recv_sem,
):
    frames, height, width, channels = x_ref.shape
    cells = height * width
    position = tuple(lax.axis_index(axis) for axis in AXES)

    def at(offsets):
        return {axis: index + offset for axis, index, offset in zip(AXES, position, offsets)}

    around = [(dz, ds, db) for dz in (0, 1) for ds in (-1, 0, 1) for db in (-1, 0, 1) if (dz, ds, db) != (0, 0, 0)]

    barrier = pltpu.get_barrier_semaphore()
    for offsets in around:
        back = tuple(-o for o in offsets)
        guarded(
            exists(position, sizes, back),
            lambda back=back: pl.semaphore_signal(barrier, inc=1, device_id=at(back), device_id_type=MESH),
        )

    x_loads = [pltpu.make_async_copy(x_hbm.at[frame], x_ref.at[frame], local_sem.at[frame]) for frame in range(2)]
    for frame in (1, 0):
        x_loads[frame].start()

    loads = []
    for layer, source in enumerate((w1_hbm, w2_hbm)):
        for offset_t in (2, 1, 0):
            copy = pltpu.make_async_copy(source.at[offset_t], weights.at[layer, offset_t], weight_sem.at[layer, offset_t])
            copy.start()
            loads.append(copy)
    loads = {(i // 3, 2 - i % 3): copy for i, copy in enumerate(loads)}
    scale_loads = [pltpu.make_async_copy(ref, scales.at[layer], local_sem.at[2 + layer]) for layer, ref in enumerate((s1_hbm, s2_hbm))]
    for copy in scale_loads:
        copy.start()

    def piece(layer, frame, main, offsets):
        dz, ds, db = offsets
        slot = frame if dz else frames + frame
        if db == 0 and ds == 0:
            src, dst, kind = main, mains.at[layer, slot], 0
        elif db == 0:
            row = height - 1 if ds > 0 else 0
            k = 0 if ds > 0 else 1
            src, dst, kind = main.at[row], rows.at[layer, slot, k], 1 + k
        else:
            side = 0 if db > 0 else 1
            src = edges.at[layer, frame, side]
            dst, kind = tiles.at[layer, slot, 1 - ds, side], 3 + 2 * (1 - ds) + side
        return pltpu.make_async_remote_copy(
            src_ref=src,
            dst_ref=dst,
            send_sem=send_sem.at[layer, slot, kind],
            recv_sem=recv_sem.at[layer, slot, kind],
            device_id=at(offsets),
            device_id_type=MESH,
        )

    def fill_edges(layer, frame, block):
        for side, column in ((0, width - 1), (1, 0)):
            picked = jnp.concatenate([block[r, column : column + 1] for r in range(height)], axis=0)
            edges[layer, frame, side, 0:height] = picked.astype(jnp.bfloat16)

    def send(layer, frame, main):
        order = sorted(around, key=lambda o: (o[0], o[2] == 0, o[1] == 0))
        for offsets in order:
            guarded(exists(position, sizes, offsets), lambda o=offsets: piece(layer, frame, main, o).start())

    def receive(layer, slot, main):
        dz = 1 if slot < frames else 0
        for offsets in around:
            if offsets[0] != dz:
                continue
            back = tuple(-o for o in offsets)
            guarded(exists(position, sizes, back), lambda o=offsets: piece(layer, slot % frames, main, o).wait_recv())

    def gather(layer, slot, block_ref):
        block = jnp.concatenate([rows[layer, slot, 0][None], block_ref[...], rows[layer, slot, 1][None]], axis=0)
        block = unpack(block, width).astype(jnp.float32)
        halo = []
        for side in range(2):
            above = tiles[layer, slot, 0, side].astype(jnp.float32)
            level = tiles[layer, slot, 1, side].astype(jnp.float32)
            below = tiles[layer, slot, 2, side].astype(jnp.float32)
            picked = [above[height - 1 : height]] + [level[r : r + 1] for r in range(height)] + [below[0:1]]
            halo.append(jnp.stack(picked, axis=0))
        column = lax.broadcasted_iota(jnp.int32, block.shape, 1)
        before = jnp.where(column == 0, halo[0], pltpu.roll(block, 1, 1))
        after = jnp.where(column == width - 1, halo[1], pltpu.roll(block, width - 1, 1))
        shifted = [part.astype(jnp.bfloat16) for part in (before, block, after)]
        pieces = [shifted[x][y : y + height].reshape(cells, channels) for y in range(3) for x in range(3)]
        taps[slot] = jnp.concatenate(pieces, axis=-1)

    def product(layer, slot, offset_t):
        return jnp.dot(taps[slot], weights[layer, offset_t], preferred_element_type=jnp.float32)

    def finish(convolved, layer):
        mean_square = jnp.sum(convolved * convolved, axis=-1, keepdims=True) * (1.0 / channels)
        normed = convolved * lax.rsqrt(mean_square + 1e-06) * scales[layer]
        return (normed / (1.0 + jnp.exp(-normed))).reshape(height, width, channels)

    for frame in (1, 0):
        x_loads[frame].wait()
        packs[0, frame] = pack(x_ref[frame])
        fill_edges(0, frame, x_ref[frame].astype(jnp.float32))

    count = jnp.int32(0)
    for offsets in around:
        condition = exists(position, sizes, offsets)
        if condition is not None:
            count = count + (1 if condition is True else condition.astype(jnp.int32))
    pl.semaphore_wait(barrier, count)

    for frame in (1, 0):
        send(0, frame, packs.at[0, frame])

    def zero(ref, condition):
        def clear():
            ref[...] = jnp.zeros_like(ref)

        if condition is None:
            clear()
        elif condition is not True:
            pl.when(jnp.logical_not(condition))(clear)

    for layer in range(2):
        for slot in range(2 * frames):
            dz = 1 if slot < frames else 0
            if dz:
                zero(mains.at[layer, slot], exists(position, sizes, (-1, 0, 0)))
            for k, ds in ((0, 1), (1, -1)):
                zero(rows.at[layer, slot, k], exists(position, sizes, (-dz, -ds, 0)))
            for k in range(3):
                for side, db in ((0, 1), (1, -1)):
                    zero(tiles.at[layer, slot, k, side], exists(position, sizes, (-dz, k - 1, -db)))
    for copy in scale_loads:
        copy.wait()

    def conv_layer(layer, source, emit):
        receive(layer, 3, source.at[1])
        gather(layer, 3, source.at[1])
        loads[layer, 2].wait()
        late = product(layer, 3, 2)
        own = lambda: (receive(layer, 2, source.at[0]), gather(layer, 2, source.at[0]))
        got = lambda slot: (receive(layer, slot, source.at[slot]), gather(layer, slot, mains.at[layer, slot]))
        if layer == 0:
            own()
            early = product(layer, 2, 2)
            loads[layer, 1].wait()
            late = late + product(layer, 2, 1)
            got(1)
            loads[layer, 0].wait()
            emit(1, finish(late + product(layer, 1, 0), layer))
            early = early + product(layer, 1, 1)
            got(0)
            emit(0, finish(early + product(layer, 0, 0), layer))
        else:
            got(1)
            loads[layer, 0].wait()
            late = late + product(layer, 1, 0)
            loads[layer, 1].wait()
            early = product(layer, 1, 1)
            own()
            early = early + product(layer, 2, 2)
            emit(1, finish(late + product(layer, 2, 1), layer))
            got(0)
            emit(0, finish(early + product(layer, 0, 0), layer))

    def emit_hidden(frame, values):
        packs[1, frame] = pack(values).astype(jnp.bfloat16)
        fill_edges(1, frame, values)
        send(1, frame, packs.at[1, frame])

    def emit_output(frame, values):
        out_ref[frame] = values.astype(jnp.bfloat16)

    conv_layer(0, packs.at[0], emit_hidden)
    conv_layer(1, packs.at[1], emit_output)

    for layer in range(2):
        for frame in (1, 0):
            for offsets in around:
                guarded(
                    exists(position, sizes, offsets),
                    lambda o=offsets: piece(layer, frame, packs.at[layer, frame], o).wait_send(),
                )


def shards(sizes, frames_in, weight_first, scale_first, weight_second, scale_second):
    frames, height, width, channels = frames_in.shape
    anywhere = pl.BlockSpec(memory_space=pl.ANY)
    lines = width * channels // 128
    flat = (3, 9 * channels, channels)
    half = jnp.bfloat16
    return pl.pallas_call(
        functools.partial(kernel, sizes),
        out_shape=pltpu.VMEM(frames_in.shape, half),
        in_specs=[anywhere] * 5,
        out_specs=pl.BlockSpec(memory_space=pltpu.VMEM),
        scratch_shapes=[
            pltpu.VMEM(frames_in.shape, half),
            pltpu.VMEM((2, 1, channels), jnp.float32),
            pltpu.VMEM((2, *flat), half),
            pltpu.VMEM((2, frames, height, lines, 128), half),
            pltpu.VMEM((2, frames, 2, 8, channels), half),
            pltpu.VMEM((2, frames, height, lines, 128), half),
            pltpu.VMEM((2, 2 * frames, 2, lines, 128), half),
            pltpu.VMEM((2, 2 * frames, 3, 2, 8, channels), half),
            pltpu.VMEM((2 * frames, height * width, 9 * channels), half),
            pltpu.SemaphoreType.DMA((4,)),
            pltpu.SemaphoreType.DMA((2, 3)),
            pltpu.SemaphoreType.DMA((2, 2 * frames, 9)),
            pltpu.SemaphoreType.DMA((2, 2 * frames, 9)),
        ],
        compiler_params=pltpu.CompilerParams(collective_id=0, has_side_effects=True),
        name="conv_block",
    )(
        frames_in,
        weight_first.reshape(flat),
        scale_first.reshape(1, channels),
        weight_second.reshape(flat),
        scale_second.reshape(1, channels),
    )


def solution(mesh):
    sizes = tuple(mesh.shape[axis] for axis in AXES)
    return jax.shard_map(
        functools.partial(shards, sizes),
        mesh=mesh,
        in_specs=(P(("groups", "frame"), "strip", "slab", None), P(), P(), P(), P()),
        out_specs=P(("groups", "frame"), "strip", "slab", None),
        check_vma=False,
    )
```
